256 devices in a mesh: seq: 32 (over y, z), head: 8 (over x, core).
Axes of the slice: x: 4, y: 4, z: 8, core: 2. Of those that a mesh axis runs over, the one named last changes fastest.
Arguments:
- features: bfloat16 [81920, 8192], P('seq', 'head'), may hold values from -75 to 75
- state_write: bfloat16 [81920, 128], P('seq'), may hold values from -6 to 6
- state_read: bfloat16 [81920, 128], P('seq'), may hold values from -1.5 to 1.5
- conv_feat: float32 [4, 8192], P(None, 'head'), may hold values from -3 to 3
- conv_state: float32 [4, 256], replicated, may hold values from -3 to 3
- log_decay: float32 [81920, 128], P('seq', 'head'), may hold values from -0.81 to 0, as said below
- skip_weight: float32 [128], P('head'), may hold values from 0.5 to 2
- norm_gain: float32 [8192], P('head'), may hold values from 0.5 to 1.5
Outputs:
- mixed_out: bfloat16 [81920, 8192], P('seq', 'head')
The draws below stay inside these ranges and needn't reach their ends.
Inputs may be any that keep to these rules, and one draw needn't show every extreme that they name: `log_decay`: every log decay is strictly negative.
All inputs are finite; a program needn't handle non-finite values.
Results may differ from the reference program's by a relative error of at most 0.0094.
Values may be sent and summed in bfloat16 or wider, within the bound.
A program may use at most 128 MiB of HBM per device.

```python
import math
import jax
import jax.numpy as jnp
from jax import lax

MIXER_HEADS = 128
HEAD_DIM = 64
STATE = 128
CONV = 4
BLOCK = 256
TOK_DEV = 2560
SEQUENCE_TOKENS = 81920
CHANNELS = 8192


def draw_features(key, part):
    key_base, key_head, key_row = jax.random.split(key, 3)
    head_ramp = jnp.arange(MIXER_HEADS, dtype=jnp.float32) / (MIXER_HEADS - 1)
    head_scale = jnp.exp(head_ramp * math.log(10.0)) * jax.random.uniform(key_head, (MIXER_HEADS,), jnp.float32, 0.8, 1.25)
    base_draw = jax.random.truncated_normal(key_base, -6.0, 6.0, (SEQUENCE_TOKENS, MIXER_HEADS, HEAD_DIM), jnp.float32)
    row_scale = jnp.exp(jax.random.uniform(key_row, (SEQUENCE_TOKENS, 1, 1), jnp.float32, 0.0, math.log(10.0)))
    values = base_draw * head_scale[None, :, None] * row_scale / 10.0
    return values.reshape(SEQUENCE_TOKENS, MIXER_HEADS * HEAD_DIM).astype(jnp.bfloat16)


def draw_log_decay(key, part):
    random_keys = jax.random.split(key, 7)
    fraction = 0.5
    is_fast = jax.random.uniform(random_keys[0], (MIXER_HEADS,), jnp.float32) < fraction
    fast_rate = jnp.exp(jax.random.uniform(random_keys[1], (MIXER_HEADS,), jnp.float32, math.log(1.0 / 50.0), math.log(1.0 / 20.0)))
    slow_rate = jax.random.uniform(random_keys[2], (MIXER_HEADS,), jnp.float32, 0.15, 0.5) / SEQUENCE_TOKENS
    base_rate = jnp.where(is_fast, fast_rate, slow_rate)
    device_blocks = SEQUENCE_TOKENS // TOK_DEV
    block_factor = jnp.exp(jax.random.uniform(random_keys[3], (device_blocks, 1, MIXER_HEADS), jnp.float32, math.log(0.5), math.log(1.5)))
    roughness = jax.random.uniform(random_keys[4], (device_blocks, TOK_DEV, MIXER_HEADS), jnp.float32, 0.5, 1.5)
    constant_level = -(base_rate[None, None, :] * block_factor * roughness).reshape(SEQUENCE_TOKENS, MIXER_HEADS)
    spike_locations = jax.random.randint(random_keys[5], (2,), 0, SEQUENCE_TOKENS)
    spike_height = jax.random.uniform(random_keys[6], (1, MIXER_HEADS), jnp.float32, 0.22, 0.69)
    token_places = jnp.arange(SEQUENCE_TOKENS, dtype=jnp.int32)
    inside_spike = jnp.any(token_places[:, None] == spike_locations[None, :], axis=1)
    return constant_level - jnp.where(inside_spike[:, None], spike_height, 0.0)


def levels(stream_key, extent, shards, low, top_value):
    def one(axis_at, parts):
        draws = jax.random.uniform(jax.random.fold_in(jax.random.fold_in(stream_key, 6), axis_at), (parts,), jnp.float32, low / len(shards), top_value / len(shards))
        return jnp.repeat(jnp.exp(draws), extent[axis_at] // parts).reshape((-1,) + (1,) * (len(extent) - axis_at - 1))

    gain = one(*shards[0])
    for cut in shards[1:]:
        gain = gain * one(*cut)
    return gain


def scatter_about(stream_key, extent, width, most, shards=(), kind=jnp.bfloat16):
    gain = levels(stream_key, extent, shards, -0.22, 0.18) if shards else 1.0
    values = jax.random.normal(stream_key, extent, jnp.float32) * width * gain
    return jnp.minimum(jnp.maximum(values, -most), most).astype(kind)


def setup_inputs(seed: int = 0) -> dict:
    splits = jax.random.split(jax.random.key(seed), 9)
    return {
        "features": draw_features(jax.random.fold_in(splits[8], 71), 0),
        "state_write": scatter_about(splits[1], (SEQUENCE_TOKENS, STATE), 1.0, 6.0, ((0, 32),)),
        "state_read": scatter_about(splits[2], (SEQUENCE_TOKENS, STATE), 0.25, 1.5, ((0, 32),)),
        "conv_feat": scatter_about(splits[3], (CONV, CHANNELS), CONV ** -0.5, 3.0, ((1, 8),), jnp.float32),
        "conv_state": scatter_about(splits[4], (CONV, 2 * STATE), CONV ** -0.5, 3.0, (), jnp.float32),
        "log_decay": draw_log_decay(jax.random.fold_in(splits[8], 71), 0),
        "skip_weight": jnp.clip(jnp.exp(math.log(2.0) - 1.3862944 * jax.random.uniform(splits[6], (MIXER_HEADS,), jnp.float32) ** levels(splits[6], (MIXER_HEADS,), ((0, 8),), -0.2, 0.2)), 0.5, 2.0),
        "norm_gain": jnp.clip(1.0 + 0.1 * jax.random.normal(splits[7], (CHANNELS,), jnp.float32), 0.5, 1.5),
    }


def conv_silu(extended, kernel_taps, length):
    summed = extended[0:length].astype(jnp.float32) * kernel_taps[0]
    for place in range(1, kernel_taps.shape[0]):
        summed = summed + extended[place:place + length].astype(jnp.float32) * kernel_taps[place]
    return jax.nn.silu(summed).astype(jnp.bfloat16)

def reference(features, state_write, state_read, conv_feat, conv_state, log_decay, skip_weight, norm_gain):
    margin = CONV - 1
    feat_conv = conv_silu(jnp.concatenate([jnp.zeros((margin, CHANNELS), jnp.bfloat16), features], axis=0), conv_feat, SEQUENCE_TOKENS)
    joined = jnp.concatenate([jnp.zeros((margin, 2 * STATE), jnp.bfloat16), jnp.concatenate([state_write, state_read], axis=1)], axis=0)
    state_conv = conv_silu(joined, conv_state, SEQUENCE_TOKENS)
    groups = SEQUENCE_TOKENS // BLOCK
    sliced = (feat_conv.reshape(groups, BLOCK, MIXER_HEADS, HEAD_DIM), state_conv[:, :STATE].reshape(groups, BLOCK, STATE), state_conv[:, STATE:].reshape(groups, BLOCK, STATE), log_decay.reshape(groups, BLOCK, MIXER_HEADS))
    causal_mask = jnp.tril(jnp.ones((BLOCK, BLOCK), dtype=bool))

    def advance(carried, pieces):
        feature_rows, write_rows, read_rows, decay_rows = pieces
        cumul_rows = jnp.cumsum(decay_rows, axis=0)
        block_total = cumul_rows[-1]
        scales = jnp.sqrt(-jnp.expm1(2.0 * decay_rows))
        scores = jnp.dot(read_rows, write_rows.T, preferred_element_type=jnp.float32)
        cum_heads = cumul_rows.T
        decay_gaps = jnp.where(causal_mask[None], cum_heads[:, :, None] - cum_heads[:, None, :], -1e+30)
        mixing = (scores[None] * jnp.exp(decay_gaps) * scales.T[:, None, :]).astype(jnp.bfloat16)
        mixing = lax.optimization_barrier(mixing).astype(jnp.float32)
        feat_wide = feature_rows.astype(jnp.float32)
        within = jnp.einsum('hts,shp->thp', mixing, feat_wide)
        start_bf = lax.optimization_barrier(carried.astype(jnp.bfloat16)).astype(jnp.float32)
        from_state = jnp.einsum('tn,hpn->thp', read_rows.astype(jnp.float32), start_bf) * jnp.exp(cumul_rows)[:, :, None]
        mixed = within + from_state + skip_weight[None, :, None] * feat_wide
        decayed = ((jnp.exp(block_total[None, :] - cumul_rows) * scales)[:, :, None] * feat_wide).astype(jnp.bfloat16)
        decayed = lax.optimization_barrier(decayed).astype(jnp.float32)
        contrib = jnp.einsum('qn,qhp->hpn', write_rows.astype(jnp.float32), decayed)
        following = jnp.exp(block_total)[:, None, None] * carried + contrib
        flat = mixed.reshape(BLOCK, CHANNELS)
        meansq = lax.optimization_barrier(jnp.mean(flat * flat, axis=1, keepdims=True))
        normed = (flat * lax.rsqrt(meansq + 1e-05) * norm_gain[None, :]).astype(jnp.bfloat16)
        return (following, normed)
    final_state, outputs = lax.scan(advance, jnp.zeros((MIXER_HEADS, HEAD_DIM, STATE), jnp.float32), sliced)
    return outputs.reshape(SEQUENCE_TOKENS, CHANNELS)
```

```python
import functools
import jax
import jax.numpy as jnp
from jax import lax
from jax.experimental import pallas as pl
from jax.experimental.pallas import tpu as pltpu
from jax.sharding import PartitionSpec as P

CHUNK = 128
LANES = 128
STATE = 128
HEAD_DIM = 64
CONV = 4
EPSILON = 1e-05
WIDE = 256
F32 = jnp.float32
BF16 = jnp.bfloat16
VMEM_LIMIT = 60 * 1024 * 1024


def dot(a, b):
    return jnp.dot(a, b, preferred_element_type=F32)


def silu(x):
    half = 0.5 * x
    return half + half * jnp.tanh(half)


def one_minus_exp(z):
    series = 1.0 + z / 9.0
    for k in range(8, 1, -1):
        series = 1.0 + (z / k) * series
    return jnp.where(z > -0.5, -z * series, 1.0 - jnp.exp(z))


def pieces(value, count):
    out = []
    for _ in range(count):
        part = value.astype(BF16).astype(F32)
        out.append(part)
        value = value - part
    return out


def halo_kernel(count, feat_ref, write_ref, read_ref, out_ref, got, send_sem, recv_sem):
    me = lax.axis_index("seq")
    right = lax.rem(me + 1, count)
    left = lax.rem(me + count - 1, count)
    barrier = pltpu.get_barrier_semaphore()
    pl.semaphore_signal(barrier, inc=1, device_id={"seq": left})
    pl.semaphore_wait(barrier, 1)
    rows = feat_ref.shape[0]
    width = feat_ref.shape[1]
    tail = pl.ds(rows - 16, 16)
    copies = []
    for k, (ref, lo, size) in enumerate(
        ((feat_ref, 0, width), (write_ref, width, STATE), (read_ref, width + STATE, STATE))
    ):
        copies.append(
            pltpu.make_async_remote_copy(
                src_ref=ref.at[tail],
                dst_ref=got.at[:, pl.ds(lo, size)],
                send_sem=send_sem.at[k],
                recv_sem=recv_sem.at[k],
                device_id={"seq": right},
            )
        )
    for copy in copies:
        copy.start()
    for copy in copies:
        copy.wait()
    value = got[...].astype(F32)
    out_ref[...] = jnp.where(me > 0, value, 0.0)[8:16]


def halo(features, state_write, state_read, count):
    width = features.shape[1] + 2 * STATE
    return pl.pallas_call(
        functools.partial(halo_kernel, count),
        out_shape=jax.ShapeDtypeStruct((8, width), F32),
        in_specs=[pl.BlockSpec(memory_space=pl.ANY)] * 3,
        out_specs=pl.BlockSpec(memory_space=pltpu.VMEM),
        scratch_shapes=[
            pltpu.VMEM((16, width), BF16),
            pltpu.SemaphoreType.DMA((3,)),
            pltpu.SemaphoreType.DMA((3,)),
        ],
        compiler_params=pltpu.CompilerParams(collective_id=0, has_side_effects=True),
        name="halo_exchange",
    )(features, state_write, state_read)


def expander(width):
    heads = width // HEAD_DIM
    row = lax.broadcasted_iota(jnp.int32, (2 * heads, width), 0)
    col = lax.broadcasted_iota(jnp.int32, (2 * heads, width), 1)
    return jnp.where(lax.rem(row, heads) == col // HEAD_DIM, 1.0, 0.0).astype(BF16)


def upper(size):
    row = lax.broadcasted_iota(jnp.int32, (size, size), 0)
    col = lax.broadcasted_iota(jnp.int32, (size, size), 1)
    return row <= col


def factors(decay, offset, tri):
    heads = decay.shape[0]
    stacked = jnp.concatenate(pieces(decay, 3), axis=0).astype(BF16)
    summed = dot(stacked, tri)
    cumul = summed[0:heads] + summed[heads : 2 * heads] + summed[2 * heads : 3 * heads]
    middle = jnp.broadcast_to(cumul[:, CHUNK // 2 - 1 : CHUNK // 2], cumul.shape)
    last = jnp.broadcast_to(cumul[:, CHUNK - 1 : CHUNK], cumul.shape)
    scale = jnp.sqrt(one_minus_exp(2.0 * decay))
    source = jnp.exp(middle - cumul) * scale
    target = jnp.exp(cumul - middle)
    after = offset + last
    lane = lax.broadcasted_iota(jnp.int32, cumul.shape, 1)
    exponent = jnp.where(
        lane == 0, middle, jnp.where(lane == 1, last - middle, jnp.where(lane == 2, offset + middle, after))
    )
    chunk = jnp.exp(exponent)
    rows = []
    for value in (source, target, chunk):
        rows += pieces(value, 2)
    rows.append(jnp.zeros((LANES - 6 * heads, CHUNK), F32))
    columns = jnp.transpose(jnp.concatenate(rows, axis=0)).astype(BF16)
    return columns, after


def local_kernel(
    steps,
    feat_ref,
    write_ref,
    read_ref,
    decay_ref,
    halo_ref,
    taps_ref,
    state_taps_ref,
    skip_ref,
    y_ref,
    r_ref,
    column_ref,
    reach_ref,
    end_ref,
    total_ref,
    ext,
    left,
    hidden,
    offset,
    spread,
    tri,
    skip_row,
):
    step = pl.program_id(0)
    width = feat_ref.shape[1]
    heads = width // HEAD_DIM
    tiles = width // LANES

    @pl.when(step == 0)
    def _():
        for tile in range(tiles + 2):
            ext[tile, 0:8, :] = halo_ref[:, tile * LANES : (tile + 1) * LANES]
        left[...] = jnp.zeros_like(left)
        hidden[...] = jnp.zeros_like(hidden)
        offset[...] = jnp.zeros_like(offset)
        spread[...] = expander(width)
        tri[...] = jnp.where(upper(CHUNK), 1.0, 0.0).astype(BF16)
        lane = lax.broadcasted_iota(jnp.int32, (8, LANES), 1)
        for tile in range(tiles):
            skip_row[:, tile * LANES : (tile + 1) * LANES] = jnp.where(
                lane < HEAD_DIM, skip_ref[2 * tile], skip_ref[2 * tile + 1]
            )

    def convolved(tile, value, taps):
        ext[tile, 8 : 8 + CHUNK, :] = value.astype(F32)
        total = ext[tile, 5 : 5 + CHUNK, :] * taps[0:1]
        for k in range(1, CONV):
            total = total + ext[tile, 5 + k : 5 + k + CHUNK, :] * taps[k : k + 1]
        ext[tile, 0:8, :] = ext[tile, CHUNK : CHUNK + 8, :]
        return silu(total)

    columns, after = factors(decay_ref[...], offset[...], tri[...])
    offset[...] = after
    column_ref[...] = columns
    chunk_rows = dot(columns[0:16, 4 * heads : 6 * heads], spread[...])
    reach_ref[0] = chunk_rows[2:3]
    enter = chunk_rows[0:1]
    leave = chunk_rows[1:2]

    written = convolved(tiles, write_ref[...], state_taps_ref[:, 0:STATE]).astype(BF16)
    reading = convolved(tiles + 1, read_ref[...], state_taps_ref[:, STATE : 2 * STATE]).astype(BF16)
    r_ref[...] = reading
    written_t = jnp.transpose(written.astype(F32)).astype(BF16)
    scores = dot(reading, written_t)
    row = lax.broadcasted_iota(jnp.int32, (CHUNK, CHUNK), 0)
    col = lax.broadcasted_iota(jnp.int32, (CHUNK, CHUNK), 1)
    scores = jnp.where(row >= col, scores, 0.0).astype(BF16)
    left[0:CHUNK, 0:CHUNK] = scores
    left[0:CHUNK, CHUNK : 2 * CHUNK] = reading
    left[CHUNK : 2 * CHUNK, 0:CHUNK] = written_t

    for block in range(width // WIDE):
        at = slice(block * WIDE, (block + 1) * WIDE)
        parts = []
        for tile in range(block * WIDE // LANES, (block + 1) * WIDE // LANES):
            lanes = slice(tile * LANES, (tile + 1) * LANES)
            parts.append(convolved(tile, feat_ref[:, lanes], taps_ref[:, lanes]))
        x = jnp.concatenate(parts, axis=1)
        source = dot(columns[:, 0 : 2 * heads], spread[:, at])
        target = dot(columns[:, 2 * heads : 4 * heads], spread[:, at])
        carried = hidden[:, at] * enter[:, at]
        right = jnp.concatenate([(x * source).astype(BF16), carried.astype(BF16)], axis=0)
        result = dot(left[...], right)
        hidden[:, at] = (carried + result[CHUNK:]) * leave[:, at]
        y_ref[:, at] = result[0:CHUNK] * target + skip_row[0:1, at] * x

    @pl.when(step == steps - 1)
    def _():
        for k in range(STATE // 16):
            for block in range(width // WIDE):
                end_ref[k * (width // WIDE) + block] = hidden[
                    k * 16 : (k + 1) * 16, block * WIDE : (block + 1) * WIDE
                ].astype(BF16)
        for block in range(width // WIDE):
            total_ref[block] = chunk_rows[3:4, block * WIDE : (block + 1) * WIDE]


def local_pass(features, state_write, state_read, decay_t, margin, conv_feat, conv_state, skip):
    length, width = features.shape
    heads = decay_t.shape[0]
    steps = length // CHUNK
    blocks = width // WIDE
    slices = STATE // 16 * blocks
    row_spec = lambda w: pl.BlockSpec((CHUNK, w), lambda i: (i, 0))
    whole = lambda shape: pl.BlockSpec(shape, lambda i: (0,) * len(shape))
    return pl.pallas_call(
        functools.partial(local_kernel, steps),
        grid=(steps,),
        out_shape=(
            jax.ShapeDtypeStruct((length, width), F32),
            jax.ShapeDtypeStruct((length, STATE), BF16),
            jax.ShapeDtypeStruct((length, LANES), BF16),
            jax.ShapeDtypeStruct((steps, 1, width), F32),
            jax.ShapeDtypeStruct((slices, 16, WIDE), BF16),
            jax.ShapeDtypeStruct((blocks, 1, WIDE), F32),
        ),
        in_specs=[
            row_spec(width),
            row_spec(STATE),
            row_spec(STATE),
            pl.BlockSpec((heads, CHUNK), lambda i: (0, i)),
            whole((8, width + 2 * STATE)),
            whole((CONV, width)),
            whole((CONV, 2 * STATE)),
            pl.BlockSpec(memory_space=pltpu.SMEM),
        ],
        out_specs=(
            row_spec(width),
            row_spec(STATE),
            row_spec(LANES),
            pl.BlockSpec((1, 1, width), lambda i: (i, 0, 0)),
            whole((slices, 16, WIDE)),
            whole((blocks, 1, WIDE)),
        ),
        scratch_shapes=[
            pltpu.VMEM((width // LANES + 2, CHUNK + 8, LANES), F32),
            pltpu.VMEM((2 * CHUNK, 2 * CHUNK), BF16),
            pltpu.VMEM((STATE, width), F32),
            pltpu.VMEM((heads, CHUNK), F32),
            pltpu.VMEM((2 * heads, width), BF16),
            pltpu.VMEM((CHUNK, CHUNK), BF16),
            pltpu.VMEM((8, width), F32),
        ],
        compiler_params=pltpu.CompilerParams(vmem_limit_bytes=VMEM_LIMIT),
        name="local_pass",
    )(features, state_write, state_read, decay_t, margin, conv_feat, conv_state, skip)


def scan_kernel(
    count, end_ref, total_ref, out_ref, ends, totals, prefix, send1, recv1, send2, recv2, send3, recv3
):
    me = lax.axis_index("seq")
    blocks = total_ref.shape[0]
    share = end_ref.shape[1]
    barrier = pltpu.get_barrier_semaphore()

    def peer(k):
        return lax.rem(me + k, count)

    def greet(k, _):
        pl.semaphore_signal(barrier, inc=1, device_id={"seq": peer(k)})
        return 0

    lax.fori_loop(1, count, greet, 0)
    pl.semaphore_wait(barrier, count - 1)

    def total_copy(to, source):
        return pltpu.make_async_remote_copy(
            src_ref=total_ref,
            dst_ref=totals.at[source],
            send_sem=send1.at[to],
            recv_sem=recv1.at[source],
            device_id={"seq": to},
        )

    def end_copy(to, source):
        return pltpu.make_async_remote_copy(
            src_ref=end_ref.at[to],
            dst_ref=ends.at[source],
            send_sem=send2.at[to],
            recv_sem=recv2.at[source],
            device_id={"seq": to},
        )

    def prefix_copy(to, source):
        return pltpu.make_async_remote_copy(
            src_ref=prefix.at[to],
            dst_ref=out_ref.at[source],
            send_sem=send3.at[to],
            recv_sem=recv3.at[source],
            device_id={"seq": to},
        )

    def post(k, _):
        total_copy(peer(k), me).start()
        end_copy(peer(k), me).start()
        return 0

    lax.fori_loop(1, count, post, 0)
    totals[me] = total_ref[...]
    ends[me] = end_ref[me]

    def send(j):
        @pl.when(j != me)
        def _():
            prefix_copy(j, me).start()

    def advance(j, carried):
        @pl.when(j != me)
        def _():
            total_copy(j, j).wait_recv()
            end_copy(j, j).wait_recv()

        following = []
        for part in range(share):
            prefix[j, part] = carried[part].astype(BF16)
            block = lax.rem(me * share + part, blocks)
            following.append(carried[part] * totals[j, block] + ends[j, part].astype(F32))

        @pl.when(j > 0)
        def _():
            send(j - 1)

        return tuple(following)

    lax.fori_loop(
        0, count, advance, tuple(jnp.zeros((16, WIDE), F32) for _ in range(share))
    )
    out_ref[me] = prefix[me]
    send(count - 1)

    def finish(k, _):
        other = peer(k)
        total_copy(other, other).wait_send()
        end_copy(other, other).wait_send()
        prefix_copy(other, other).wait_send()
        prefix_copy(other, other).wait_recv()
        return 0

    lax.fori_loop(1, count, finish, 0)


def scan(end, total, count):
    slices = end.shape[0]
    blocks = total.shape[0]
    share = slices // count
    dma = pltpu.SemaphoreType.DMA((count,))
    vmem = pl.BlockSpec(memory_space=pltpu.VMEM)
    return pl.pallas_call(
        functools.partial(scan_kernel, count),
        out_shape=jax.ShapeDtypeStruct((count, share, 16, WIDE), BF16),
        in_specs=[vmem, vmem],
        out_specs=vmem,
        scratch_shapes=[
            pltpu.VMEM((count, share, 16, WIDE), BF16),
            pltpu.VMEM((count, blocks, 1, WIDE), F32),
            pltpu.VMEM((count, share, 16, WIDE), BF16),
            dma, dma, dma, dma, dma, dma,
        ],
        compiler_params=pltpu.CompilerParams(collective_id=1, has_side_effects=True),
        name="state_scan",
    )(end.reshape(count, share, 16, WIDE), total)


def correct_kernel(y_ref, r_ref, column_ref, reach_ref, carried_ref, mixed_ref, square_ref, spread):
    width = y_ref.shape[1]
    heads = width // HEAD_DIM
    blocks = width // WIDE

    @pl.when(pl.program_id(0) == 0)
    def _():
        spread[...] = expander(width)

    reading = r_ref[...]
    columns = column_ref[:, 2 * heads : 4 * heads]
    squares = jnp.zeros((CHUNK, LANES), F32)
    for block in range(blocks):
        at = slice(block * WIDE, (block + 1) * WIDE)
        carried = jnp.concatenate(
            [carried_ref[k * blocks + block] for k in range(STATE // 16)], axis=0
        ).astype(F32)
        state = (carried * reach_ref[0, :, at]).astype(BF16)
        mixed = y_ref[:, at] + dot(columns, spread[:, at]) * dot(reading, state)
        mixed_ref[:, at] = mixed.astype(BF16)
        for tile in range(WIDE // LANES):
            part = mixed[:, tile * LANES : (tile + 1) * LANES]
            squares = squares + part * part
    square_ref[0] = jnp.sum(jnp.transpose(squares), axis=0, keepdims=True)


def correct(y, reading, columns, reach, carried):
    length, width = y.shape
    steps = length // CHUNK
    row_spec = lambda w: pl.BlockSpec((CHUNK, w), lambda i: (i, 0))
    carried = carried.reshape(-1, 16, WIDE)
    return pl.pallas_call(
        correct_kernel,
        grid=(steps,),
        out_shape=(
            jax.ShapeDtypeStruct((length, width), BF16),
            jax.ShapeDtypeStruct((steps, 1, CHUNK), F32),
        ),
        in_specs=[
            row_spec(width),
            row_spec(STATE),
            row_spec(LANES),
            pl.BlockSpec((1, 1, width), lambda i: (i, 0, 0)),
            pl.BlockSpec(carried.shape, lambda i: (0, 0, 0)),
        ],
        out_specs=(row_spec(width), pl.BlockSpec((1, 1, CHUNK), lambda i: (i, 0, 0))),
        scratch_shapes=[pltpu.VMEM((2 * width // HEAD_DIM, width), BF16)],
        compiler_params=pltpu.CompilerParams(vmem_limit_bytes=VMEM_LIMIT),
        name="correct",
    )(y, reading, columns, reach, carried)


def sums_kernel(count, channels, square_ref, out_ref, got, send_sem, recv_sem):
    me = lax.axis_index("head")
    barrier = pltpu.get_barrier_semaphore()
    others = [lax.rem(me + k, count) for k in range(1, count)]
    for other in others:
        pl.semaphore_signal(barrier, inc=1, device_id={"head": other})
    pl.semaphore_wait(barrier, count - 1)

    def copy(to, source, k):
        return pltpu.make_async_remote_copy(
            src_ref=square_ref,
            dst_ref=got.at[source],
            send_sem=send_sem.at[k],
            recv_sem=recv_sem.at[source],
            device_id={"head": to},
        )

    for k, other in enumerate(others):
        copy(other, me, k).start()
    got[me] = square_ref[...]
    for k, other in enumerate(others):
        copy(other, other, k).wait_recv()
    total = got[0]
    for k in range(1, count):
        total = total + got[k]
    out_ref[...] = lax.rsqrt(total / channels + EPSILON)
    for k, other in enumerate(others):
        copy(other, me, k).wait_send()


def sums(squares, count, channels):
    vmem = pl.BlockSpec(memory_space=pltpu.VMEM)
    return pl.pallas_call(
        functools.partial(sums_kernel, count, channels),
        out_shape=jax.ShapeDtypeStruct(squares.shape, F32),
        in_specs=[vmem],
        out_specs=vmem,
        scratch_shapes=[
            pltpu.VMEM((count,) + squares.shape, F32),
            pltpu.SemaphoreType.DMA((count - 1,)),
            pltpu.SemaphoreType.DMA((count,)),
        ],
        compiler_params=pltpu.CompilerParams(collective_id=2, has_side_effects=True),
        name="square_sums",
    )(squares)


def final_kernel(mixed_ref, scale_ref, gain_ref, out_ref):
    width = mixed_ref.shape[1]
    for k in range(mixed_ref.shape[0] // CHUNK):
        rows = slice(k * CHUNK, (k + 1) * CHUNK)
        scale = jnp.transpose(jnp.broadcast_to(scale_ref[k], (CHUNK, CHUNK)))
        for tile in range(width // LANES):
            at = slice(tile * LANES, (tile + 1) * LANES)
            out_ref[rows, at] = (mixed_ref[rows, at].astype(F32) * scale * gain_ref[:, at]).astype(BF16)


def final(mixed, scales, gain):
    length, width = mixed.shape
    group = 2
    rows = group * CHUNK
    return pl.pallas_call(
        final_kernel,
        grid=(length // rows,),
        out_shape=jax.ShapeDtypeStruct((length, width), BF16),
        in_specs=[
            pl.BlockSpec((rows, width), lambda i: (i, 0)),
            pl.BlockSpec((group, 1, CHUNK), lambda i: (i, 0, 0)),
            pl.BlockSpec((1, width), lambda i: (0, 0)),
        ],
        out_specs=pl.BlockSpec((rows, width), lambda i: (i, 0)),
        compiler_params=pltpu.CompilerParams(vmem_limit_bytes=VMEM_LIMIT),
        name="final_scale",
    )(mixed, scales, gain)


def on_device(
    seq_count, head_count, features, state_write, state_read, conv_feat, conv_state, log_decay, skip_weight, norm_gain
):
    margin = halo(features, state_write, state_read, seq_count)
    y, reading, columns, reach, end, total = local_pass(
        features, state_write, state_read, log_decay.T, margin, conv_feat, conv_state, skip_weight
    )
    carried = scan(end, total, seq_count)
    mixed, squares = correct(y, reading, columns, reach, carried)
    channels = features.shape[1] * head_count
    scales = sums(squares, head_count, channels)
    return final(mixed, scales, norm_gain.reshape(1, -1))


def solution(mesh):
    placed = (
        P("seq", "head"),
        P("seq", None),
        P("seq", None),
        P(None, "head"),
        P(),
        P("seq", "head"),
        P("head"),
        P("head"),
    )
    body = functools.partial(on_device, mesh.shape["seq"], mesh.shape["head"])
    return jax.shard_map(
        body, mesh=mesh, in_specs=placed, out_specs=P("seq", "head"), check_vma=False
    )
```

```python
import functools
import jax
import jax.numpy as jnp
from jax import lax
from jax.experimental import pallas as pl
from jax.experimental.pallas import tpu as pltpu
from jax.sharding import PartitionSpec as P

CHUNK = 128
LANES = 128
STATE = 128
HEAD_DIM = 64
CONV = 4
EPSILON = 1e-05
WIDE = 256
F32 = jnp.float32
BF16 = jnp.bfloat16
VMEM_LIMIT = 64000 * 1024
MIXER_VMEM = 64000 * 1024


def dot(a, b):
    return jnp.dot(a, b, preferred_element_type=F32)


def one_minus_exp(z):
    series = 1.0 + z / 9.0
    for k in range(8, 1, -1):
        series = 1.0 + (z / k) * series
    return jnp.where(z > -0.5, -z * series, 1.0 - jnp.exp(z))


def pieces(value, count):
    out = []
    for _ in range(count):
        part = value.astype(BF16).astype(F32)
        out.append(part)
        value = value - part
    return out


def expander(width):
    heads = width // HEAD_DIM
    row = lax.broadcasted_iota(jnp.int32, (2 * heads, width), 0)
    col = lax.broadcasted_iota(jnp.int32, (2 * heads, width), 1)
    return jnp.where(lax.rem(row, heads) == col // HEAD_DIM, 1.0, 0.0).astype(BF16)


def upper(size):
    row = lax.broadcasted_iota(jnp.int32, (size, size), 0)
    col = lax.broadcasted_iota(jnp.int32, (size, size), 1)
    return row <= col


def factors(decay, offset, tri):
    heads = decay.shape[0]
    stacked = jnp.concatenate(pieces(decay, 3), axis=0).astype(BF16)
    summed = dot(stacked, tri)
    cumul = summed[0:heads] + summed[heads : 2 * heads] + summed[2 * heads : 3 * heads]
    middle = jnp.broadcast_to(cumul[:, CHUNK // 2 - 1 : CHUNK // 2], cumul.shape)
    last = jnp.broadcast_to(cumul[:, CHUNK - 1 : CHUNK], cumul.shape)
    scale = jnp.sqrt(one_minus_exp(2.0 * decay))
    source = jnp.exp(middle - cumul) * scale
    target = jnp.exp(cumul - middle)
    after = offset + last
    lane = lax.broadcasted_iota(jnp.int32, cumul.shape, 1)
    exponent = jnp.where(
        lane == 0, middle, jnp.where(lane == 1, last - middle, jnp.where(lane == 2, offset + middle, after))
    )
    chunk = jnp.exp(exponent)
    rows = []
    for value in (source, target, chunk):
        rows += pieces(value, 2)
    rows.append(jnp.zeros((LANES - 6 * heads, CHUNK), F32))
    columns = jnp.transpose(jnp.concatenate(rows, axis=0)).astype(BF16)
    return columns, after


HALVES = 2
MARGIN = 16


def mixer_kernel(
    seq_count,
    head_count,
    feat_ref,
    write_ref,
    read_ref,
    decay_ref,
    taps_ref,
    state_taps_ref,
    skip_ref,
    mixed_ref,
    scale_ref,
    feat,
    pair,
    columns,
    rows,
    left,
    written_t,
    ext,
    hidden,
    xs,
    xb,
    enter,
    local,
    mixed,
    spread,
    skip_row,
    total,
    totals,
    ends,
    got_ends,
    prefix,
    carried,
    carried_wide,
    squares,
    square_rows,
    got_squares,
    feat_sem,
    pair_sem,
    out_sem,
    halo_send,
    halo_recv,
    total_send,
    total_recv,
    end_send,
    end_recv,
    prefix_send,
    prefix_recv,
    sum_send,
    sum_recv,
):
    length, width = feat_ref.shape
    steps = length // CHUNK
    heads = width // HEAD_DIM
    half = width // HALVES
    half_tiles = half // LANES
    tiles = width // LANES
    share = ends.shape[2]
    me = lax.axis_index("seq")
    my_head = lax.axis_index("head")
    right = lax.rem(me + 1, seq_count)

    def peer(k):
        return lax.rem(me + k, seq_count)

    other_heads = [lax.rem(my_head + k, head_count) for k in range(1, head_count)]
    barrier = pltpu.get_barrier_semaphore()

    def greet(k, _):
        pl.semaphore_signal(barrier, inc=1, device_id={"seq": peer(k)})
        return 0

    lax.fori_loop(1, seq_count, greet, 0)
    for other in other_heads:
        pl.semaphore_signal(barrier, inc=1, device_id={"head": other})

    def feat_copy(c):
        at = pl.multiple_of(c * CHUNK, CHUNK)
        return pltpu.make_async_copy(
            feat_ref.at[pl.ds(at, CHUNK)], feat.at[pl.ds(MARGIN + at, CHUNK)], feat_sem.at[c]
        )

    def pair_copy(ref, k):
        return pltpu.make_async_copy(
            ref, pair.at[pl.ds(MARGIN, length), pl.ds(k * STATE, STATE)], pair_sem.at[k]
        )

    pair_copy(write_ref, 0).start()
    pair_copy(read_ref, 1).start()

    def fetch(c, _):
        feat_copy(c).start()
        return 0

    lax.fori_loop(0, steps, fetch, 0)

    spread[...] = expander(width)
    lane = lax.broadcasted_iota(jnp.int32, (8, LANES), 1)
    for tile in range(tiles):
        skip_row[:, tile * LANES : (tile + 1) * LANES] = jnp.where(
            lane < HEAD_DIM, skip_ref[2 * tile], skip_ref[2 * tile + 1]
        )
    tri = jnp.where(upper(CHUNK), 1.0, 0.0).astype(BF16)

    def prepare(c, offset):
        at = pl.multiple_of(c * CHUNK, CHUNK)
        value, after = factors(decay_ref[:, pl.ds(at, CHUNK)], offset, tri)
        columns[pl.ds(at, CHUNK), :] = value
        rows[c] = dot(value[0:16, 4 * heads : 6 * heads], spread[...])[0:8]
        return after

    lax.fori_loop(0, steps, prepare, jnp.zeros((heads, CHUNK), F32))
    rows[steps] = jnp.ones((8, width), F32)
    for tile in range(tiles):
        total[tile] = rows[steps - 1, 3:4, tile * LANES : (tile + 1) * LANES]

    pl.semaphore_wait(barrier, seq_count + head_count - 2)

    edge = pl.ds(length - MARGIN, MARGIN)
    top = pl.ds(0, MARGIN)

    def halo_copy(ref, to, k):
        return pltpu.make_async_remote_copy(
            src_ref=ref.at[edge],
            dst_ref=to,
            send_sem=halo_send.at[k],
            recv_sem=halo_recv.at[k],
            device_id={"seq": right},
        )

    halos = (
        halo_copy(write_ref, pair.at[top, pl.ds(0, STATE)], 0),
        halo_copy(read_ref, pair.at[top, pl.ds(STATE, STATE)], 1),
        halo_copy(feat_ref, feat.at[top], 2),
    )
    for copy in halos:
        copy.start()

    def total_copy(to, source):
        return pltpu.make_async_remote_copy(
            src_ref=total,
            dst_ref=totals.at[source],
            send_sem=total_send.at[to],
            recv_sem=total_recv.at[source],
            device_id={"seq": to},
        )

    def send_total(k, _):
        total_copy(peer(k), me).start()
        return 0

    lax.fori_loop(1, seq_count, send_total, 0)
    totals[me] = total[...]

    def convolved(tile, value, taps):
        ext[tile] = value.astype(F32)
        low = MARGIN - CONV + 1
        summed = ext[tile, low : low + CHUNK, :] * taps[0:1]
        for k in range(1, CONV):
            summed = summed + ext[tile, low + k : low + k + CHUNK, :] * taps[k : k + 1]
        return summed + summed * jnp.tanh(summed)

    pair_copy(write_ref, 0).wait()
    pair_copy(read_ref, 1).wait()
    state_taps = 0.5 * state_taps_ref[...]

    def coefficients(c):
        at = pl.multiple_of(c * CHUNK, CHUNK)
        window = pl.ds(at, CHUNK + MARGIN)
        written = convolved(0, pair[window, 0:STATE], state_taps[:, 0:STATE]).astype(BF16)
        reading = convolved(1, pair[window, STATE : 2 * STATE], state_taps[:, STATE:]).astype(BF16)
        flipped = jnp.transpose(written.astype(F32)).astype(BF16)
        scores = dot(reading, flipped)
        row = lax.broadcasted_iota(jnp.int32, (CHUNK, CHUNK), 0)
        col = lax.broadcasted_iota(jnp.int32, (CHUNK, CHUNK), 1)
        left[c, :, 0:CHUNK] = jnp.where(row >= col, scores, 0.0).astype(BF16)
        left[c, :, CHUNK : 2 * CHUNK] = reading
        written_t[c] = flipped

    def later_coefficients(c, _):
        coefficients(c)
        return 0

    lax.fori_loop(1, steps, later_coefficients, 0)
    for copy in halos:
        copy.wait()

    @pl.when(me == 0)
    def _():
        pair[0:MARGIN, :] = jnp.zeros((MARGIN, 2 * STATE), BF16)
        feat[0:MARGIN, :] = jnp.zeros((MARGIN, width), BF16)

    coefficients(0)

    def advance_states(part):
        hidden[...] = jnp.zeros_like(hidden)

        def one(c, _):
            if part == 0:
                feat_copy(c).wait()
            at = pl.multiple_of(c * CHUNK, CHUNK)
            window = pl.ds(at, CHUNK + MARGIN)
            here = pl.ds(at, CHUNK)
            for block in range(half // WIDE):
                own = slice(block * WIDE, (block + 1) * WIDE)
                lanes = slice(part * half + block * WIDE, part * half + (block + 1) * WIDE)
                pieces_x = []
                for tile in range(WIDE // LANES):
                    lo = lanes.start + tile * LANES
                    tile_lanes = slice(lo, lo + LANES)
                    pieces_x.append(
                        convolved(
                            own.start // LANES + tile, feat[window, tile_lanes], 0.5 * taps_ref[:, tile_lanes]
                        )
                    )
                x = jnp.concatenate(pieces_x, axis=1)
                xb[here, lanes] = x.astype(BF16)
                source = dot(columns[here, 0 : 2 * heads], spread[:, lanes])
                scaled = (x * source).astype(BF16)
                xs[here, lanes] = scaled
                state = hidden[:, own]
                enter[here, lanes] = state.astype(BF16)
                factor = rows[c, 1:2, lanes] * rows[c + 1, 0:1, lanes]
                hidden[:, own] = (state + dot(written_t[c], scaled)) * factor
            return 0

        lax.fori_loop(0, steps, one, 0)
        for tile in range(STATE // 16 * half_tiles):
            r, q = tile // half_tiles, tile % half_tiles
            ends[part, tile // share, tile % share] = hidden[
                r * 16 : (r + 1) * 16, q * LANES : (q + 1) * LANES
            ].astype(BF16)

    def end_copy(part, to, source):
        return pltpu.make_async_remote_copy(
            src_ref=ends.at[part, to],
            dst_ref=got_ends.at[part, source],
            send_sem=end_send.at[part, to],
            recv_sem=end_recv.at[part, source],
            device_id={"seq": to},
        )

    def prefix_copy(part, to, source):
        return pltpu.make_async_remote_copy(
            src_ref=prefix.at[part, to],
            dst_ref=carried.at[part, source],
            send_sem=prefix_send.at[part, to],
            recv_sem=prefix_recv.at[part, source],
            device_id={"seq": to},
        )

    def send_ends(part):
        def one(k, _):
            end_copy(part, peer(k), me).start()
            return 0

        lax.fori_loop(1, seq_count, one, 0)
        got_ends[part, me] = ends[part, me]

    def scan_shards(part):
        def send(j):
            @pl.when(j != me)
            def _():
                prefix_copy(part, j, me).start()

        def one(j, running):
            @pl.when(j != me)
            def _():
                if part == 0:
                    total_copy(j, j).wait_recv()
                end_copy(part, j, j).wait_recv()

            following = []
            for k in range(share):
                prefix[part, j, k] = running[k].astype(BF16)
                tile = part * half_tiles + lax.rem(me * share + k, half_tiles)
                following.append(running[k] * totals[j, tile] + got_ends[part, j, k].astype(F32))

            @pl.when(j > 0)
            def _():
                send(j - 1)

            return tuple(following)

        lax.fori_loop(0, seq_count, one, tuple(jnp.zeros((16, LANES), F32) for _ in range(share)))
        carried[part, me] = prefix[part, me]
        send(seq_count - 1)

    def within(part):
        def one(c, _):
            here = pl.ds(pl.multiple_of(c * CHUNK, CHUNK), CHUNK)
            for block in range(half // WIDE):
                lanes = slice(part * half + block * WIDE, part * half + (block + 1) * WIDE)
                operand = jnp.concatenate([xs[here, lanes], enter[here, lanes]], axis=0)
                target = dot(columns[here, 2 * heads : 4 * heads], spread[:, lanes])
                local[here, lanes] = (
                    dot(left[c], operand) * target + skip_row[0:1, lanes] * xb[here, lanes].astype(F32)
                )
            return 0

        lax.fori_loop(0, steps, one, 0)

    def receive(part):
        def one(k, _):
            other = peer(k)
            prefix_copy(part, other, other).wait_recv()
            return 0

        lax.fori_loop(1, seq_count, one, 0)
        for tile in range(STATE // 16 * half_tiles):
            r, q = tile // half_tiles, tile % half_tiles
            carried_wide[r * 16 : (r + 1) * 16, q * LANES : (q + 1) * LANES] = carried[
                part, tile // share, tile % share
            ].astype(F32)

    def out_copy(c):
        at = pl.multiple_of(c * CHUNK, CHUNK)
        return pltpu.make_async_copy(mixed.at[pl.ds(at, CHUNK)], mixed_ref.at[pl.ds(at, CHUNK)], out_sem.at[c])

    def correct(part):
        def one(c, _):
            here = pl.ds(pl.multiple_of(c * CHUNK, CHUNK), CHUNK)
            reading = left[c, :, CHUNK : 2 * CHUNK]
            summed = jnp.zeros((CHUNK, LANES), F32)
            for block in range(half // WIDE):
                own = slice(block * WIDE, (block + 1) * WIDE)
                lanes = slice(part * half + block * WIDE, part * half + (block + 1) * WIDE)
                state = (carried_wide[:, own] * rows[c, 2:3, lanes]).astype(BF16)
                target = dot(columns[here, 2 * heads : 4 * heads], spread[:, lanes])
                value = local[here, lanes] + target * dot(reading, state)
                mixed[here, lanes] = value.astype(BF16)
                for tile in range(WIDE // LANES):
                    one_tile = value[:, tile * LANES : (tile + 1) * LANES]
                    summed = summed + one_tile * one_tile
            if part == 0:
                squares[c] = summed
            else:
                square_rows[c] = jnp.sum(jnp.transpose(squares[c] + summed), axis=0, keepdims=True)

                @pl.when(c > 0)
                def _():
                    out_copy(c - 1).start()

            return 0

        lax.fori_loop(0, steps, one, 0)

    advance_states(0)
    send_ends(0)
    advance_states(1)
    send_ends(1)
    within(0)
    scan_shards(0)
    within(1)
    scan_shards(1)
    receive(0)
    correct(0)
    receive(1)
    correct(1)
    out_copy(steps - 1).start()

    def sum_copy(to, source, k):
        return pltpu.make_async_remote_copy(
            src_ref=square_rows,
            dst_ref=got_squares.at[source],
            send_sem=sum_send.at[k],
            recv_sem=sum_recv.at[source],
            device_id={"head": to},
        )

    for k, other in enumerate(other_heads):
        sum_copy(other, my_head, k).start()
    got_squares[my_head] = square_rows[...]

    def finish(k, _):
        other = peer(k)
        total_copy(other, other).wait_send()
        for part in range(HALVES):
            end_copy(part, other, other).wait_send()
            prefix_copy(part, other, other).wait_send()
        return 0

    lax.fori_loop(1, seq_count, finish, 0)

    def drain(c, _):
        out_copy(c).wait()
        return 0

    lax.fori_loop(0, steps, drain, 0)
    for k, other in enumerate(other_heads):
        sum_copy(other, other, k).wait_recv()
    summed = got_squares[0]
    for k in range(1, head_count):
        summed = summed + got_squares[k]
    scale_ref[...] = lax.rsqrt(summed / (width * head_count) + EPSILON)
    for k, other in enumerate(other_heads):
        sum_copy(other, my_head, k).wait_send()


def mixer(features, state_write, state_read, decay_t, conv_feat, conv_state, skip, seq_count, head_count):
    length, width = features.shape
    heads = decay_t.shape[0]
    steps = length // CHUNK
    half = width // HALVES
    share = STATE // 16 * (half // LANES) // seq_count
    dma = lambda *shape: pltpu.SemaphoreType.DMA(shape)
    anywhere = pl.BlockSpec(memory_space=pl.ANY)
    vmem = pl.BlockSpec(memory_space=pltpu.VMEM)
    shards = pltpu.VMEM((HALVES, seq_count, share, 16, LANES), BF16)
    return pl.pallas_call(
        functools.partial(mixer_kernel, seq_count, head_count),
        out_shape=(
            jax.ShapeDtypeStruct((length, width), BF16),
            jax.ShapeDtypeStruct((steps, 1, CHUNK), F32),
        ),
        in_specs=[anywhere] * 3 + [vmem] * 3 + [pl.BlockSpec(memory_space=pltpu.SMEM)],
        out_specs=(anywhere, vmem),
        scratch_shapes=[
            pltpu.VMEM((MARGIN + length, width), BF16),
            pltpu.VMEM((MARGIN + length, 2 * STATE), BF16),
            pltpu.VMEM((length, LANES), BF16),
            pltpu.VMEM((steps + 1, 8, width), F32),
            pltpu.VMEM((steps, CHUNK, 2 * CHUNK), BF16),
            pltpu.VMEM((steps, STATE, CHUNK), BF16),
            pltpu.VMEM((half // LANES, CHUNK + MARGIN, LANES), F32),
            pltpu.VMEM((STATE, half), F32),
            pltpu.VMEM((length, width), BF16),
            pltpu.VMEM((length, width), BF16),
            pltpu.VMEM((length, width), BF16),
            pltpu.VMEM((length, width), F32),
            pltpu.VMEM((length, width), BF16),
            pltpu.VMEM((2 * heads, width), BF16),
            pltpu.VMEM((8, width), F32),
            pltpu.VMEM((width // LANES, 1, LANES), F32),
            pltpu.VMEM((seq_count, width // LANES, 1, LANES), F32),
            shards,
            shards,
            shards,
            shards,
            pltpu.VMEM((STATE, half), F32),
            pltpu.VMEM((steps, CHUNK, LANES), F32),
            pltpu.VMEM((steps, 1, CHUNK), F32),
            pltpu.VMEM((head_count, steps, 1, CHUNK), F32),
            dma(steps),
            dma(2),
            dma(steps),
            dma(3),
            dma(3),
            dma(seq_count),
            dma(seq_count),
            dma(HALVES, seq_count),
            dma(HALVES, seq_count),
            dma(HALVES, seq_count),
            dma(HALVES, seq_count),
            dma(head_count - 1),
            dma(head_count),
        ],
        compiler_params=pltpu.CompilerParams(
            collective_id=0, has_side_effects=True, vmem_limit_bytes=MIXER_VMEM
        ),
        name="mixer",
    )(features, state_write, state_read, decay_t, conv_feat, conv_state, skip)


def final_kernel(mixed_ref, scale_ref, gain_ref, out_ref):
    width = mixed_ref.shape[1]
    for k in range(mixed_ref.shape[0] // CHUNK):
        rows = slice(k * CHUNK, (k + 1) * CHUNK)
        scale = jnp.transpose(jnp.broadcast_to(scale_ref[k], (CHUNK, CHUNK)))
        for tile in range(width // LANES):
            at = slice(tile * LANES, (tile + 1) * LANES)
            out_ref[rows, at] = (mixed_ref[rows, at].astype(F32) * scale * gain_ref[:, at]).astype(BF16)


def final(mixed, scales, gain):
    length, width = mixed.shape
    group = next(k for k in (5, 2, 1) if length // CHUNK % k == 0)
    rows = group * CHUNK
    return pl.pallas_call(
        final_kernel,
        grid=(length // rows,),
        out_shape=jax.ShapeDtypeStruct((length, width), BF16),
        in_specs=[
            pl.BlockSpec((rows, width), lambda i: (i, 0)),
            pl.BlockSpec((group, 1, CHUNK), lambda i: (i, 0, 0)),
            pl.BlockSpec((1, width), lambda i: (0, 0)),
        ],
        out_specs=pl.BlockSpec((rows, width), lambda i: (i, 0)),
        compiler_params=pltpu.CompilerParams(vmem_limit_bytes=VMEM_LIMIT),
        name="final_scale",
    )(mixed, scales, gain)


def on_device(
    seq_count, head_count, features, state_write, state_read, conv_feat, conv_state, log_decay, skip_weight, norm_gain
):
    mixed, scales = mixer(
        features,
        state_write,
        state_read,
        log_decay.T,
        conv_feat,
        conv_state,
        skip_weight,
        seq_count,
        head_count,
    )
    return final(mixed, scales, norm_gain.reshape(1, -1))


def solution(mesh):
    placed = (
        P("seq", "head"),
        P("seq", None),
        P("seq", None),
        P(None, "head"),
        P(),
        P("seq", "head"),
        P("head"),
        P("head"),
    )
    body = functools.partial(on_device, mesh.shape["seq"], mesh.shape["head"])
    return jax.shard_map(
        body, mesh=mesh, in_specs=placed, out_specs=P("seq", "head"), check_vma=False
    )
```
